256 devices in a mesh: req: 64 (over x, z, core), tensor: 4 (over y).
Axes of the slice: x: 4, y: 4, z: 8, core: 2. Of those that a mesh axis runs over, the one named last changes fastest.
Arguments:
- stream: bfloat16 [65536, 2048], P('req', 'tensor'), may hold values from -64 to 64
- target_row: int32 [65536], P('req'), may hold values from -1 to 65535, as said below
- segment_ids: int32 [65536], P('req'), may hold values from -1 to 63, as said below
- cache_slot: int32 [65536], P('req'), may hold values from -1 to 2047, as said below
- norm_gain: bfloat16 [2048], replicated, may hold values from 0.099609375 to 1.8984375
- norm_bias: bfloat16 [2048], replicated, may hold values from -3 to 3
- projection: bfloat16 [2048, 3, 2048], P(None, None, 'tensor'), may hold values from -1 to 1
- output_weight: bfloat16 [2048, 2048], P('tensor'), may hold values from -0.125 to 0.125
- cache_pool: bfloat16 [131072, 2, 2048], P('req', None, 'tensor'), may hold values from -6 to 6
Outputs:
- mixed: bfloat16 [65536, 2048], P('req', 'tensor')
- new_pool: bfloat16 [131072, 2, 2048], P('req', None, 'tensor')
The draws below stay inside these ranges and needn't reach their ends.
Inputs may be any that keep to these rules, and one draw needn't show every extreme that they name: `target_row`: every live row of the request layout is named by exactly one stream row and no other row is named. A device names at most 16 rows of any one device; in every draw some device receives exactly 16 rows from every device and its 1024 rows are all live. `segment_ids`: within one device's 1024 rows the numbers start at 0 on the first row, rise by one at each new request and never fall; a request's rows are consecutive and never cross devices; -1 only on the rows after the last request. A device holds at most 64 requests, and in every draw some device holds exactly that many. `cache_slot`: live rows of one device have distinct slots; a request's rows fill its pages in order, each page being 16 consecutive slots beginning at a multiple of 16; -1 exactly on rows where segment_ids is -1.
All inputs are finite; a program needn't handle non-finite values.
Results may differ from the reference program's by a relative error of at most 0.008.
Values may be sent and summed in bfloat16 or wider, within the bound.
No kernel may reach another device: no remote copies, remote signals or barrier semaphores. Data moves between devices by JAX's collectives and lax.ppermute only.
A program may use at most 128 MiB of HBM per device.

```python
import math
import jax
import jax.numpy as jnp
from jax import lax

D = 2048
HEADS = 8
HDIM = 256
ROT = 64
PAGE = 16
TOK_DEV = 1024
POOL_ROWS = 2048
TOKENS = 65536
N_REQ = 64
N_TENSOR = 4


def layout_tables(key):
    subkeys = jax.random.split(jax.random.fold_in(key, 17), 8)
    cap_rows = TOK_DEV // N_REQ
    device_ids = jnp.arange(N_REQ, dtype=jnp.int32)
    row_ids = jnp.arange(TOK_DEV, dtype=jnp.int32)
    used_rows = jax.random.randint(subkeys[0], (N_REQ,), 2 * TOK_DEV // 5, TOK_DEV + 1)
    full_device = jax.random.randint(subkeys[1], (), 0, N_REQ)
    used_rows = jnp.where((device_ids == full_device) | (device_ids == N_REQ - 1), TOK_DEV, used_rows)
    is_live = row_ids[None, :] < used_rows[:, None]
    window = row_ids // PAGE
    start_offset = jax.random.randint(subkeys[2], (N_REQ, TOK_DEV // PAGE), 0, PAGE)
    start_offset = start_offset.at[:, 0].set(0)
    opens = jax.random.randint(subkeys[3], (N_REQ, TOK_DEV // PAGE), 0, 8) == 0
    opens = opens | (device_ids == full_device)[:, None]
    opens = opens.at[:, 0].set(True)
    candidate = (row_ids % PAGE)[None, :] == start_offset[:, window]
    is_start = candidate & opens[:, window] & is_live
    segment = jnp.where(is_live, jnp.cumsum(is_start.astype(jnp.int32), axis=1) - 1, -1)
    first_row = lax.cummax(jnp.where(is_start, row_ids[None, :], 0), axis=1)
    position = row_ids[None, :] - first_row
    page_start = (is_live & (position % PAGE == 0)).astype(jnp.int32)
    page_index = jnp.maximum(jnp.cumsum(page_start, axis=1) - 1, 0)
    page_order = jax.vmap(lambda subkey: jax.random.permutation(subkey, POOL_ROWS // PAGE))(jax.random.split(subkeys[4], N_REQ))
    slot = jnp.take_along_axis(page_order.astype(jnp.int32), page_index.astype(jnp.int32), axis=1) * PAGE + position % PAGE
    slot = jnp.where(is_live, slot, -1)
    offsets = jax.random.permutation(subkeys[5], N_REQ).astype(jnp.int32)
    slot_order = jax.vmap(lambda subkey: jax.random.permutation(subkey, TOK_DEV))(jax.random.split(subkeys[6], N_REQ)).astype(jnp.int32)
    slot_inverse = jnp.argsort(slot_order, axis=1).astype(jnp.int32)
    stream_order = jax.vmap(lambda subkey: jax.random.permutation(subkey, TOK_DEV))(jax.random.split(subkeys[7], N_REQ)).astype(jnp.int32)
    block_number = stream_order // cap_rows
    receiver = (device_ids[:, None] - offsets[block_number]) % N_REQ
    dest_local = slot_inverse[receiver, stream_order]
    sends_row = dest_local < used_rows[receiver]
    target = jnp.where(sends_row, receiver * TOK_DEV + dest_local, -1)
    return (segment.astype(jnp.int32), position.astype(jnp.int32), slot.astype(jnp.int32), target.astype(jnp.int32), is_live)


def draw_target_row(key, part):
    tables = layout_tables(key)
    return tables[3].reshape(-1).astype(jnp.int32)


def draw_segment_ids(key, part):
    tables = layout_tables(key)
    return tables[0].reshape(-1).astype(jnp.int32)


def draw_cache_slot(key, part):
    tables = layout_tables(key)
    return tables[2].reshape(-1).astype(jnp.int32)


def draw_stream(key, part):
    subkeys = jax.random.split(jax.random.fold_in(key, 29), 1)
    values = jnp.clip(jax.random.normal(subkeys[0], (TOKENS, D), jnp.float32), -4.0, 4.0)
    return values.astype(jnp.bfloat16)


def draw_projection(key, part):
    subkeys = jax.random.split(jax.random.fold_in(key, 41), 1)
    head_width = HEADS * HDIM
    base = jnp.clip(jax.random.normal(subkeys[0], (D, 3, head_width), jnp.float32), -4.0, 4.0) / math.sqrt(D)
    return jnp.clip(base, -1.0, 1.0).astype(jnp.bfloat16)


def block_levels(own_key, extent, cuts, least, top_value):
    def one(dim, parts):
        draws = jax.random.uniform(jax.random.fold_in(jax.random.fold_in(own_key, 6), dim), (parts,), jnp.float32, least / len(cuts), top_value / len(cuts))
        return jnp.repeat(jnp.exp(draws), extent[dim] // parts).reshape((-1,) + (1,) * (len(extent) - dim - 1))

    gain = one(*cuts[0])
    for cut in cuts[1:]:
        gain = gain * one(*cut)
    return gain


def bell_draw(key, extent, scale, bound, cuts=(), held_as=jnp.bfloat16):
    drawn = scale * jax.random.normal(key, extent, jnp.float32)
    if cuts:
        drawn = drawn * block_levels(key, extent, cuts, -0.22, 0.18)
    return jnp.clip(drawn, -bound, bound).astype(held_as)


def setup_inputs(seed: int = 0) -> dict:
    key_list = jax.random.split(jax.random.key(seed), 10)
    return {
        "stream": draw_stream(jax.random.fold_in(key_list[9], 71), 0),
        "target_row": draw_target_row(jax.random.fold_in(key_list[9], 71), 0),
        "segment_ids": draw_segment_ids(jax.random.fold_in(key_list[9], 71), 0),
        "cache_slot": draw_cache_slot(jax.random.fold_in(key_list[9], 71), 0),
        "norm_gain": jnp.clip(1.0 + 0.18 * jax.random.normal(key_list[4], (D,), jnp.float32), 0.099609375, 1.8984375).astype(jnp.bfloat16),
        "norm_bias": bell_draw(key_list[5], (D,), 0.5, 3.0),
        "projection": draw_projection(jax.random.fold_in(key_list[9], 71), 0),
        "output_weight": bell_draw(key_list[7], (HEADS * HDIM, D), (HEADS * HDIM) ** -0.5, 0.125, ((0, 4),)),
        "cache_pool": bell_draw(key_list[8], (N_REQ * POOL_ROWS, 2, HEADS * HDIM), 1.0, 6.0, ((0, 64), (2, 4))),
    }


norm_epsilon = 1e-05
masked_score = -1e+30
rotary_base = 10000.0

def layer_norm(values, norm_gain, norm_bias):
    widened = values.astype(jnp.float32)
    row_mean = lax.optimization_barrier(jnp.mean(widened, axis=-1, keepdims=True))
    centred = widened - row_mean
    row_var = lax.optimization_barrier(jnp.mean(centred * centred, axis=-1, keepdims=True))
    scaled = centred * lax.rsqrt(row_var + norm_epsilon)
    return (scaled * norm_gain.astype(jnp.float32) + norm_bias.astype(jnp.float32)).astype(jnp.bfloat16)

def positions(segment):
    row_ids = jnp.arange(segment.shape[0], dtype=jnp.int32)
    earlier = jnp.concatenate([jnp.full((1,), -2, jnp.int32), segment[:-1].astype(jnp.int32)])
    is_start = segment.astype(jnp.int32) != earlier
    first_row = lax.cummax(jnp.where(is_start, row_ids, 0), axis=0)
    return row_ids - first_row

def rotary(heads_in, position):
    half_rot = ROT // 2
    exponent = jnp.arange(half_rot, dtype=jnp.float32) * (2.0 / ROT)
    inverse_freq = 1.0 / rotary_base ** exponent
    angles = position.astype(jnp.float32)[:, None] * inverse_freq[None, :]
    cosine = jnp.cos(angles)[:, None, :]
    sine_part = jnp.sin(angles)[:, None, :]
    widened = heads_in.astype(jnp.float32)
    row_count = widened.shape[0]
    head_count = widened.shape[1]
    paired = widened[..., :ROT].reshape(row_count, head_count, half_rot, 2)
    even_part = paired[..., 0]
    odd_part = paired[..., 1]
    turned = jnp.stack([even_part * cosine - odd_part * sine_part, odd_part * cosine + even_part * sine_part], axis=-1)
    turned = turned.reshape(row_count, head_count, ROT)
    return jnp.concatenate([turned, widened[..., ROT:]], axis=-1).astype(jnp.bfloat16)

def device_layer(placed, segment, slots, pool_part, norm_gain, norm_bias, projection, output_weight):
    row_count = placed.shape[0]
    head_width = HEADS * HDIM
    score_scale = 1.0 / math.sqrt(HDIM)
    is_live = segment >= 0
    position = positions(segment)
    normed = layer_norm(placed, norm_gain, norm_bias)
    projected = jnp.dot(normed, projection.reshape(D, 3 * head_width), preferred_element_type=jnp.float32).astype(jnp.bfloat16)
    projected = projected.reshape(row_count, 3, HEADS, HDIM)
    queries = rotary(projected[:, 0], position)
    keys_rot = rotary(projected[:, 1], position)
    values_all = projected[:, 2]
    scores = jnp.einsum('qhd,khd->hqk', queries.astype(jnp.float32), keys_rot.astype(jnp.float32)) * score_scale
    row_ids = jnp.arange(row_count, dtype=jnp.int32)
    allowed = (segment[:, None] == segment[None, :]) & (row_ids[None, :] <= row_ids[:, None])
    scores = jnp.where(allowed[None], scores, masked_score)
    top_score = lax.optimization_barrier(jnp.max(scores, axis=-1, keepdims=True))
    raised = jnp.where(allowed[None], jnp.exp(scores - top_score), 0.0)
    row_total = lax.optimization_barrier(jnp.sum(raised, axis=-1, keepdims=True))
    weights = (raised / row_total).astype(jnp.bfloat16)
    context = jnp.einsum('hqk,khd->qhd', weights.astype(jnp.float32), values_all.astype(jnp.float32)).astype(jnp.bfloat16)
    grouped = context.reshape(row_count, N_TENSOR, head_width // N_TENSOR).astype(jnp.float32)
    out_groups = output_weight.reshape(N_TENSOR, head_width // N_TENSOR, D).astype(jnp.float32)
    head_partial = jnp.einsum('tgf,gfd->gtd', grouped, out_groups).astype(jnp.bfloat16)
    head_partial = lax.optimization_barrier(head_partial)
    summed = lax.optimization_barrier(jnp.sum(head_partial.astype(jnp.float32), axis=0))
    mixed_rows = jnp.where(is_live[:, None], placed.astype(jnp.float32) + summed, 0.0).astype(jnp.bfloat16)
    key_value = jnp.stack([keys_rot.reshape(row_count, head_width), values_all.reshape(row_count, head_width)], axis=1)
    where_slot = jnp.where(is_live, slots, pool_part.shape[0])
    new_pool = pool_part.at[where_slot].set(key_value, mode='drop')
    return (mixed_rows, new_pool)

def reference(stream, target_row, segment_ids, cache_slot, norm_gain, norm_bias, projection, output_weight, cache_pool):
    head_width = HEADS * HDIM
    where_to = jnp.where(target_row >= 0, target_row, TOKENS)
    placed = jnp.zeros((TOKENS, D), jnp.bfloat16).at[where_to].set(stream, mode='drop')

    def one_device(packed):
        return device_layer(packed[0], packed[1], packed[2], packed[3], norm_gain, norm_bias, projection, output_weight)
    mixed_rows, new_pool = lax.map(one_device, (placed.reshape(N_REQ, TOK_DEV, D), segment_ids.reshape(N_REQ, TOK_DEV), cache_slot.reshape(N_REQ, TOK_DEV), cache_pool.reshape(N_REQ, POOL_ROWS, 2, head_width)))
    return (mixed_rows.reshape(TOKENS, D), new_pool.reshape(N_REQ * POOL_ROWS, 2, head_width))
```

```python
import functools
import math

import jax
import jax.numpy as jnp
from jax import lax
from jax.experimental import pallas as pl
from jax.experimental.pallas import tpu as pltpu
from jax.sharding import PartitionSpec as P

HDIM = 256
ROT = 64
LANES = 128
CHUNKS = 4

norm_epsilon = 1e-05
masked_score = -1e30
rotary_base = 10000.0

bf16 = jnp.bfloat16
f32 = jnp.float32
i32 = jnp.int32


def iota(shape, dim):
    return lax.broadcasted_iota(i32, shape, dim)


def hot(condition):
    return jnp.where(condition, 1.0, 0.0).astype(bf16)


def dot(a, b):
    return jnp.dot(a, b, preferred_element_type=f32)


def dot_nt(a, b):
    return lax.dot_general(a, b, (((1,), (1,)), ((), ())), preferred_element_type=f32)


def whole(shape):
    zeros = (0,) * len(shape)
    return pl.BlockSpec(shape, lambda *_: zeros)


def pack_kernel(target_ref, stream_ref, packed_ref, *, peers):
    row_count = target_ref.shape[1]
    cap = row_count // peers
    width = stream_ref.shape[1]
    parts = width // LANES
    target = target_ref[...]
    sends = target >= 0
    receiver = jnp.where(sends, target // row_count, peers)
    local = jnp.where(sends, target - receiver * row_count + 1, 0)
    onehot = jnp.where(iota((peers, row_count), 0) == receiver, 1.0, 0.0)
    upper = hot(iota((LANES, LANES), 0) < iota((LANES, LANES), 1))
    carry = jnp.zeros((peers, 1), f32)
    ranks = []
    for start in range(0, row_count, LANES):
        block = onehot[:, start : start + LANES]
        before = dot(block.astype(bf16), upper) + carry
        ranks.append(jnp.sum(block * before, axis=0, keepdims=True))
        carry = carry + jnp.sum(block, axis=1, keepdims=True)
    rank = jnp.concatenate(ranks, axis=1).astype(i32)
    slot = jnp.where(sends, receiver * cap + rank, -1)
    high = local // 32
    low = local - high * 32
    lane = iota((LANES, row_count), 0)
    table = dot_nt((onehot * high.astype(f32)).astype(bf16), hot(lane == rank)) + dot_nt(
        (onehot * low.astype(f32)).astype(bf16), hot(lane == rank + cap)
    )
    repeat = hot(iota((peers * 8, peers), 0) // 8 == iota((peers * 8, peers), 1))
    packed_ref[:, cap * parts :, :] = (
        dot(repeat, table.astype(bf16)).reshape(peers, 8, LANES).astype(bf16)
    )
    step = 256
    for start in range(0, row_count, step):
        chosen = hot(iota((step, row_count), 0) + start == slot)
        rows = dot(chosen, stream_ref[...])
        first = start // cap
        for part in range(parts):
            packed_ref[first : first + step // cap, part * cap : (part + 1) * cap, :] = (
                rows[:, part * LANES : (part + 1) * LANES].reshape(step // cap, cap, LANES).astype(bf16)
            )


def pack(target, stream, peers):
    row_count, width = stream.shape
    cap = row_count // peers
    return pl.pallas_call(
        functools.partial(pack_kernel, peers=peers),
        out_shape=jax.ShapeDtypeStruct((peers, cap * (width // LANES) + 8, LANES), bf16),
        name="pack",
    )(target.reshape(1, row_count), stream)


def unpack_kernel(got_ref, *placed_refs):
    peers = got_ref.shape[0]
    chunk, width = placed_refs[0].shape
    row_count = chunk * len(placed_refs)
    cap = row_count // peers
    parts = width // LANES
    tables = got_ref[:, cap * parts :, :].astype(f32).reshape(peers * 8, LANES).astype(bf16)
    table = dot(hot(iota((peers, peers * 8), 1) == 8 * iota((peers, peers * 8), 0)), tables)
    table = table.astype(bf16)
    lane = iota((LANES, row_count), 0)
    rank = iota((LANES, row_count), 1) % cap
    value = 32.0 * dot(table, hot(lane == rank)) + dot(table, hot(lane == rank + cap))
    owner = iota((peers, row_count), 1) // cap == iota((peers, row_count), 0)
    arrived = jnp.sum(jnp.where(owner, value, 0.0), axis=0, keepdims=True).astype(i32) - 1
    for number, placed_ref in enumerate(placed_refs):
        chosen = hot(iota((chunk, row_count), 0) + number * chunk == arrived)
        for part in range(parts):
            rows = got_ref[:, part * cap : (part + 1) * cap, :].reshape(row_count, LANES)
            placed_ref[:, part * LANES : (part + 1) * LANES] = dot(chosen, rows).astype(bf16)


def unpack(got, row_count, width):
    chunk = row_count // CHUNKS
    return pl.pallas_call(
        unpack_kernel,
        out_shape=[jax.ShapeDtypeStruct((chunk, width), bf16)] * CHUNKS,
        name="unpack",
    )(got)


def layer_kernel(number, group_ref, *refs):
    (own, left, right, far_top, far_bottom, weight, gain, bias, cosine, sine, segment_row, segment_col), rest = (
        refs[:12],
        refs[12:],
    )
    past_keys, past_values, (context, keys_out, values_out) = (
        rest[:number],
        rest[number : 2 * number],
        rest[2 * number :],
    )
    chunk, width = own.shape
    groups = weight.shape[0] // width
    me = group_ref[0]
    pieces = [
        own[...].astype(f32),
        left[...].astype(f32),
        jnp.concatenate([far_top[...], far_bottom[...]], axis=0).astype(f32),
        right[...].astype(f32),
    ]
    total = sum(jnp.sum(piece, axis=1, keepdims=True) for piece in pieces)
    mean = total * (1.0 / (width * groups))
    centred = [piece - mean for piece in pieces]
    spread = sum(jnp.sum(piece * piece, axis=1, keepdims=True) for piece in centred)
    scale = lax.rsqrt(spread * (1.0 / (width * groups)) + norm_epsilon)
    projected = None
    for offset, piece in enumerate(centred):
        source = lax.rem(me + groups - offset, groups)
        place = pl.ds(pl.multiple_of(source * width, width), width)
        normed = (piece * scale * gain[:, place].astype(f32) + bias[:, place].astype(f32)).astype(bf16)
        partial = dot(normed, weight[place, :])
        projected = partial if projected is None else projected + partial
    projected = projected.astype(bf16)
    cos_part = cosine[...]
    sin_part = sine[...]
    even = iota((chunk, LANES), 1) % 2 == 0

    def turn(head):
        lead = head[:, :LANES].astype(f32)
        swapped = jnp.where(even, pltpu.roll(lead, LANES - 1, 1), pltpu.roll(lead, 1, 1))
        turned = (lead * cos_part + swapped * sin_part).astype(bf16)
        return jnp.concatenate([turned, head[:, LANES:]], axis=1)

    segment = segment_col[...]
    allowed = []
    for block in range(number + 1):
        same = segment_row[:, block * chunk : (block + 1) * chunk] == segment
        if block == number:
            same = same & (iota((chunk, chunk), 1) <= iota((chunk, chunk), 0))
        allowed.append(same)
    score_scale = 1.0 / math.sqrt(HDIM)
    for head in range(width // HDIM):
        cols = slice(head * HDIM, (head + 1) * HDIM)
        query = turn(projected[:, head * HDIM : (head + 1) * HDIM])
        key = turn(projected[:, width + head * HDIM : width + (head + 1) * HDIM])
        value = projected[:, 2 * width + head * HDIM : 2 * width + (head + 1) * HDIM]
        keys_out[:, cols] = key
        values_out[:, cols] = value
        keys = [ref[:, cols] for ref in past_keys] + [key]
        values = [ref[:, cols] for ref in past_values] + [value]
        scores = [
            jnp.where(mask, dot_nt(query, block) * score_scale, masked_score)
            for mask, block in zip(allowed, keys)
        ]
        top = functools.reduce(jnp.maximum, [jnp.max(s, axis=1, keepdims=True) for s in scores])
        raised = [jnp.where(mask, jnp.exp(s - top), 0.0) for mask, s in zip(allowed, scores)]
        row_total = sum(jnp.sum(r, axis=1, keepdims=True) for r in raised)
        inverse = 1.0 / row_total
        mixed = sum(dot((r * inverse).astype(bf16), v) for r, v in zip(raised, values))
        context[:, cols] = mixed.astype(bf16)


def layer(number, group, pieces, weight, gain, bias, cosine, sine, segment_row, segment_col, keys, values):
    chunk, width = pieces[0].shape
    by_chunk = lambda columns: pl.BlockSpec((chunk, columns), lambda i, g: (number, 0))
    rows = jax.ShapeDtypeStruct((chunk, width), bf16)
    return pl.pallas_call(
        functools.partial(layer_kernel, number),
        grid_spec=pltpu.PrefetchScalarGridSpec(
            num_scalar_prefetch=1,
            grid=(1,),
            in_specs=[whole(piece.shape) for piece in pieces]
            + [whole(weight.shape), whole(gain.shape), whole(bias.shape)]
            + [by_chunk(LANES), by_chunk(LANES), whole(segment_row.shape), by_chunk(1)]
            + [whole(rows.shape)] * (2 * number),
            out_specs=[whole(rows.shape)] * 3,
        ),
        out_shape=[rows] * 3,
        name="layer",
    )(group, *pieces, weight, gain, bias, cosine, sine, segment_row, segment_col, *keys, *values)


def finish_kernel(*refs):
    own, left, right, far_top, far_bottom, w_own, w_left, w_far, w_right, placed, segment_col = refs[:11]
    mixed = refs[-1]
    total = dot(own[...], w_own[...]) + dot(left[...], w_left[...]) + dot(right[...], w_right[...])
    total = total + dot(jnp.concatenate([far_top[...], far_bottom[...]], axis=0), w_far[...])
    mixed[...] = jnp.where(segment_col[...] >= 0, placed[...].astype(f32) + total, 0.0).astype(bf16)


def finish(number, pieces, weights, placed, segment_col, buffer):
    chunk, width = placed.shape
    row_count = segment_col.shape[0]
    given = [*pieces, *weights, placed]
    specs = [whole(array.shape) for array in given] + [pl.BlockSpec((chunk, 1), lambda i: (number, 0))]
    given.append(segment_col)
    aliases = {}
    if buffer is not None:
        aliases = {len(given): 0}
        given.append(buffer)
        specs.append(pl.BlockSpec(memory_space=pl.ANY))
    return pl.pallas_call(
        finish_kernel,
        grid=(1,),
        in_specs=specs,
        out_specs=pl.BlockSpec((chunk, width), lambda i: (number, 0)),
        out_shape=jax.ShapeDtypeStruct((row_count, width), bf16),
        input_output_aliases=aliases,
        name="finish",
    )(*given)


def shift(values, distance):
    size = lax.axis_size("tensor")
    return lax.ppermute(values, "tensor", [(i, (i + distance) % size) for i in range(size)])


def gather_pieces(own):
    half = own.shape[0] // 2
    left = shift(own, 1)
    right = shift(own, -1)
    return own, left, right, shift(left[:half], 1), shift(right[half:], -1)


def rotary_tables(segment_ids):
    row_count = segment_ids.shape[0]
    row_ids = jnp.arange(row_count, dtype=i32)
    earlier = (segment_ids[:, None] == segment_ids[None, :]) & (row_ids[None, :] < row_ids[:, None])
    position = jnp.sum(earlier.astype(i32), axis=1)
    lane = jnp.arange(LANES, dtype=i32)
    exponent = (lane // 2).astype(f32) * (2.0 / ROT)
    inverse_freq = 1.0 / rotary_base**exponent
    angles = position.astype(f32)[:, None] * inverse_freq[None, :]
    turned = (lane < ROT)[None, :]
    sign = jnp.where(lane % 2 == 0, -1.0, 1.0)[None, :]
    return jnp.where(turned, jnp.cos(angles), 1.0), jnp.where(turned, jnp.sin(angles) * sign, 0.0)


def shards(
    stream,
    target_row,
    segment_ids,
    cache_slot,
    norm_gain,
    norm_bias,
    projection,
    output_weight,
    cache_pool,
):
    peers = lax.axis_size("req")
    groups = lax.axis_size("tensor")
    me = lax.axis_index("tensor")
    row_count, width = stream.shape
    depth = projection.shape[0]

    packed = pack(target_row, stream, peers)
    got = lax.all_to_all(packed, "req", split_axis=0, concat_axis=0, tiled=True)

    weight = projection.reshape(depth, projection.shape[1] * width)
    cosine, sine = rotary_tables(segment_ids)
    segment_row = segment_ids.reshape(1, row_count)
    segment_col = segment_ids.reshape(row_count, 1)
    gain = norm_gain.reshape(1, depth)
    bias = norm_bias.reshape(1, depth)
    out_weights = []
    for offset in range(groups):
        target = lax.rem(me + offset, groups)
        block = lax.dynamic_slice_in_dim(output_weight, target * width, width, axis=1)
        out_weights.append(block if offset == 0 else shift(block, offset))
    group = me.astype(i32).reshape(1)

    placed = unpack(got, row_count, width)
    gathered = [gather_pieces(chunk) for chunk in placed]
    keys, values, contexts = [], [], []
    for number in range(CHUNKS):
        context, key, value = layer(
            number, group, gathered[number], weight, gain, bias, cosine, sine, segment_row, segment_col, keys, values
        )
        keys.append(key)
        values.append(value)
        contexts.append(gather_pieces(context))
    mixed = None
    for number in range(CHUNKS):
        mixed = finish(number, contexts[number], out_weights, placed[number], segment_col, mixed)

    live_slot = jnp.where(segment_ids >= 0, cache_slot, -1)
    slot_ids = jnp.arange(cache_pool.shape[0], dtype=i32)
    matches = slot_ids[:, None] == live_slot[None, :]
    chosen = matches.astype(bf16)
    written = [
        dot(chosen, jnp.concatenate(rows, axis=0)).astype(bf16) for rows in (keys, values)
    ]
    new_pool = jnp.where(
        jnp.any(matches, axis=1)[:, None, None], jnp.stack(written, axis=1), cache_pool
    )
    return (mixed, new_pool)


def solution(mesh):
    in_specs = (
        P("req", "tensor"),
        P("req"),
        P("req"),
        P("req"),
        P(),
        P(),
        P(None, None, "tensor"),
        P("tensor", None),
        P("req", None, "tensor"),
    )
    out_specs = (P("req", "tensor"), P("req", None, "tensor"))
    return jax.shard_map(shards, mesh=mesh, in_specs=in_specs, out_specs=out_specs, check_vma=False)
```

```python
import functools
import math

import jax
import jax.numpy as jnp
from jax import lax
from jax.experimental import pallas as pl
from jax.experimental.pallas import tpu as pltpu
from jax.sharding import PartitionSpec as P

HDIM = 256
ROT = 64
LANES = 128
CHUNKS = 2

norm_epsilon = 1e-05
masked_score = -1e30
rotary_base = 10000.0

bf16 = jnp.bfloat16
f32 = jnp.float32
i32 = jnp.int32


def iota(shape, dim):
    return lax.broadcasted_iota(i32, shape, dim)


def hot(condition):
    return jnp.where(condition, 1.0, 0.0).astype(bf16)


def dot(a, b):
    return jnp.dot(a, b, preferred_element_type=f32)


def dot_nt(a, b):
    return lax.dot_general(a, b, (((1,), (1,)), ((), ())), preferred_element_type=f32)


def whole(shape):
    zeros = (0,) * len(shape)
    return pl.BlockSpec(shape, lambda *_: zeros)


def pack_kernel(target_ref, stream_ref, packed_ref, *, peers):
    row_count = target_ref.shape[1]
    cap = row_count // peers
    width = stream_ref.shape[1]
    parts = width // LANES
    target = target_ref[...]
    sends = target >= 0
    receiver = jnp.where(sends, target // row_count, peers)
    local = jnp.where(sends, target - receiver * row_count + 1, 0)
    onehot = jnp.where(iota((peers, row_count), 0) == receiver, 1.0, 0.0)
    upper = hot(iota((LANES, LANES), 0) < iota((LANES, LANES), 1))
    carry = jnp.zeros((peers, 1), f32)
    ranks = []
    for start in range(0, row_count, LANES):
        block = onehot[:, start : start + LANES]
        before = dot(block.astype(bf16), upper) + carry
        ranks.append(jnp.sum(block * before, axis=0, keepdims=True))
        carry = carry + jnp.sum(block, axis=1, keepdims=True)
    rank = jnp.concatenate(ranks, axis=1).astype(i32)
    slot = jnp.where(sends, receiver * cap + rank, -1)
    high = local // 32
    low = local - high * 32
    lane = iota((LANES, row_count), 0)
    table = dot_nt((onehot * high.astype(f32)).astype(bf16), hot(lane == rank)) + dot_nt(
        (onehot * low.astype(f32)).astype(bf16), hot(lane == rank + cap)
    )
    repeat = hot(iota((peers * 8, peers), 0) // 8 == iota((peers * 8, peers), 1))
    packed_ref[:, cap * parts :, :] = (
        dot(repeat, table.astype(bf16)).reshape(peers, 8, LANES).astype(bf16)
    )
    step = 256
    for start in range(0, row_count, step):
        chosen = hot(iota((step, row_count), 0) + start == slot)
        rows = dot(chosen, stream_ref[...])
        first = start // cap
        for part in range(parts):
            packed_ref[first : first + step // cap, part * cap : (part + 1) * cap, :] = (
                rows[:, part * LANES : (part + 1) * LANES].reshape(step // cap, cap, LANES).astype(bf16)
            )


def pack(target, stream, peers):
    row_count, width = stream.shape
    cap = row_count // peers
    return pl.pallas_call(
        functools.partial(pack_kernel, peers=peers),
        out_shape=jax.ShapeDtypeStruct((peers, cap * (width // LANES) + 8, LANES), bf16),
        name="pack",
    )(target.reshape(1, row_count), stream)


def unpack_kernel(got_ref, *placed_refs):
    peers = got_ref.shape[0]
    chunk, width = placed_refs[0].shape
    row_count = chunk * len(placed_refs)
    cap = row_count // peers
    parts = width // LANES
    tables = got_ref[:, cap * parts :, :].astype(f32).reshape(peers * 8, LANES).astype(bf16)
    table = dot(hot(iota((peers, peers * 8), 1) == 8 * iota((peers, peers * 8), 0)), tables)
    table = table.astype(bf16)
    lane = iota((LANES, row_count), 0)
    rank = iota((LANES, row_count), 1) % cap
    value = 32.0 * dot(table, hot(lane == rank)) + dot(table, hot(lane == rank + cap))
    owner = iota((peers, row_count), 1) // cap == iota((peers, row_count), 0)
    arrived = jnp.sum(jnp.where(owner, value, 0.0), axis=0, keepdims=True).astype(i32) - 1
    for number, placed_ref in enumerate(placed_refs):
        chosen = hot(iota((chunk, row_count), 0) + number * chunk == arrived)
        for part in range(parts):
            rows = got_ref[:, part * cap : (part + 1) * cap, :].reshape(row_count, LANES)
            placed_ref[:, part * LANES : (part + 1) * LANES] = dot(chosen, rows).astype(bf16)


def unpack(got, row_count, width):
    chunk = row_count // CHUNKS
    return pl.pallas_call(
        unpack_kernel,
        out_shape=[jax.ShapeDtypeStruct((chunk, width), bf16)] * CHUNKS,
        name="unpack",
    )(got)


def layer_kernel(number, group_ref, *refs):
    own, left, right, far_top, far_bottom, *weights = refs[:8]
    gain, bias, cosine, sine, segment_row, segment_col = refs[8:14]
    rest = refs[14:]
    past_keys, past_values, (context, keys_out, values_out) = (
        rest[:number],
        rest[number : 2 * number],
        rest[2 * number :],
    )
    chunk, width = own.shape
    groups = gain.shape[1] // width
    me = group_ref[0]
    pieces = [
        own[...].astype(f32),
        left[...].astype(f32),
        jnp.concatenate([far_top[...], far_bottom[...]], axis=0).astype(f32),
        right[...].astype(f32),
    ]
    total = sum(jnp.sum(piece, axis=1, keepdims=True) for piece in pieces)
    mean = total * (1.0 / (width * groups))
    centred = [piece - mean for piece in pieces]
    spread = sum(jnp.sum(piece * piece, axis=1, keepdims=True) for piece in centred)
    scale = lax.rsqrt(spread * (1.0 / (width * groups)) + norm_epsilon)
    projected = [0.0, 0.0, 0.0]
    for offset, piece in enumerate(centred):
        source = lax.rem(me + groups - offset, groups)
        place = pl.ds(pl.multiple_of(source * width, width), width)
        normed = (piece * scale * gain[:, place].astype(f32) + bias[:, place].astype(f32)).astype(bf16)
        projected = [total + dot(normed, weight[place, :]) for total, weight in zip(projected, weights)]
    raw_queries, raw_keys, raw_values = [total.astype(bf16) for total in projected]
    cos_part = cosine[...]
    sin_part = sine[...]
    even = iota((chunk, LANES), 1) % 2 == 0

    def turn(head):
        lead = head[:, :LANES].astype(f32)
        swapped = jnp.where(even, pltpu.roll(lead, LANES - 1, 1), pltpu.roll(lead, 1, 1))
        turned = (lead * cos_part + swapped * sin_part).astype(bf16)
        return jnp.concatenate([turned, head[:, LANES:]], axis=1)

    segment = segment_col[...]
    allowed = []
    for block in range(number + 1):
        same = segment_row[:, block * chunk : (block + 1) * chunk] == segment
        if block == number:
            same = same & (iota((chunk, chunk), 1) <= iota((chunk, chunk), 0))
        allowed.append(same)
    score_scale = 1.0 / math.sqrt(HDIM)
    for head in range(width // HDIM):
        cols = slice(head * HDIM, (head + 1) * HDIM)
        query = turn(raw_queries[:, cols])
        key = turn(raw_keys[:, cols])
        value = raw_values[:, cols]
        keys_out[:, cols] = key
        values_out[:, cols] = value
        keys = [ref[:, cols] for ref in past_keys] + [key]
        values = [ref[:, cols] for ref in past_values] + [value]
        scores = [
            jnp.where(mask, dot_nt(query, block) * score_scale, masked_score)
            for mask, block in zip(allowed, keys)
        ]
        top = functools.reduce(jnp.maximum, [jnp.max(s, axis=1, keepdims=True) for s in scores])
        raised = [jnp.where(mask, jnp.exp(s - top), 0.0) for mask, s in zip(allowed, scores)]
        row_total = sum(jnp.sum(r, axis=1, keepdims=True) for r in raised)
        inverse = 1.0 / row_total
        mixed = sum(dot((r * inverse).astype(bf16), v) for r, v in zip(raised, values))
        context[:, cols] = mixed.astype(bf16)


def layer(number, group, pieces, weights, gain, bias, cosine, sine, segment_row, segment_col, keys, values):
    chunk, width = pieces[0].shape
    by_chunk = lambda columns: pl.BlockSpec((chunk, columns), lambda i, g: (number, 0))
    rows = jax.ShapeDtypeStruct((chunk, width), bf16)
    return pl.pallas_call(
        functools.partial(layer_kernel, number),
        grid_spec=pltpu.PrefetchScalarGridSpec(
            num_scalar_prefetch=1,
            grid=(1,),
            in_specs=[whole(piece.shape) for piece in pieces]
            + [whole(array.shape) for array in (*weights, gain, bias)]
            + [by_chunk(LANES), by_chunk(LANES), whole(segment_row.shape), by_chunk(1)]
            + [whole(rows.shape)] * (2 * number),
            out_specs=[whole(rows.shape)] * 3,
        ),
        out_shape=[rows] * 3,
        compiler_params=pltpu.CompilerParams(vmem_limit_bytes=40 << 20),
        name="layer",
    )(group, *pieces, *weights, gain, bias, cosine, sine, segment_row, segment_col, *keys, *values)


def finish_kernel(*refs):
    own, left, right, far_top, far_bottom, w_own, w_left, w_far, w_right, placed, segment_col = refs[:11]
    mixed = refs[-1]
    total = dot(own[...], w_own[...]) + dot(left[...], w_left[...]) + dot(right[...], w_right[...])
    total = total + dot(jnp.concatenate([far_top[...], far_bottom[...]], axis=0), w_far[...])
    mixed[...] = jnp.where(segment_col[...] >= 0, placed[...].astype(f32) + total, 0.0).astype(bf16)


def finish(number, pieces, weights, placed, segment_col, buffer):
    chunk, width = placed.shape
    row_count = segment_col.shape[0]
    given = [*pieces, *weights, placed]
    specs = [whole(array.shape) for array in given] + [pl.BlockSpec((chunk, 1), lambda i: (number, 0))]
    given.append(segment_col)
    aliases = {}
    if buffer is not None:
        aliases = {len(given): 0}
        given.append(buffer)
        specs.append(pl.BlockSpec(memory_space=pl.ANY))
    return pl.pallas_call(
        finish_kernel,
        grid=(1,),
        in_specs=specs,
        out_specs=pl.BlockSpec((chunk, width), lambda i: (number, 0)),
        out_shape=jax.ShapeDtypeStruct((row_count, width), bf16),
        input_output_aliases=aliases,
        compiler_params=pltpu.CompilerParams(vmem_limit_bytes=16 << 20),
        name="finish",
    )(*given)


def pool_kernel(slot_ref, old_ref, *refs):
    *row_refs, out_ref, spread_ref = refs
    row_count = slot_ref.shape[1]
    half = len(row_refs) // 2
    width = row_refs[0].shape[1]
    parts = width // LANES
    chunk = row_refs[0].shape[0]
    per_slot = 2 * parts
    step = out_ref.shape[0] // per_slot
    chosen = hot(iota((step, row_count), 0) + pl.program_id(0) * step == slot_ref[...])
    found = jnp.sum(chosen.astype(f32), axis=1, keepdims=True)
    for which in range(2):
        rows = sum(
            dot(chosen[:, number * chunk : (number + 1) * chunk], ref[...])
            for number, ref in enumerate(row_refs[which * half : (which + 1) * half])
        )
        for part in range(parts):
            spread_ref[pl.ds(2 * part + which, step, stride=per_slot), :] = rows[
                :, part * LANES : (part + 1) * LANES
            ]
    repeat = hot(iota((step * per_slot, step), 0) // per_slot == iota((step * per_slot, step), 1))
    written = dot(repeat, jnp.broadcast_to(found, (step, LANES)).astype(bf16))
    out_ref[...] = jnp.where(written > 0.5, spread_ref[...].astype(bf16), old_ref[...])


def write_pool(live_slot, cache_pool, keys, values):
    slots, pair, width = cache_pool.shape
    parts = width // LANES
    per_slot = pair * parts
    step = 256
    row_count = live_slot.shape[0]
    flat = cache_pool.reshape(slots, pair, parts, LANES).transpose(0, 2, 1, 3).reshape(slots * per_slot, LANES)
    block = pl.BlockSpec((step * per_slot, LANES), lambda i: (i, 0))
    rows = [*keys, *values]
    out = pl.pallas_call(
        pool_kernel,
        grid=(slots // step,),
        in_specs=[whole((1, row_count)), block] + [whole(array.shape) for array in rows],
        out_specs=block,
        out_shape=jax.ShapeDtypeStruct(flat.shape, bf16),
        scratch_shapes=[pltpu.VMEM((step * per_slot, LANES), f32)],
        compiler_params=pltpu.CompilerParams(vmem_limit_bytes=32 << 20),
        name="pool",
    )(live_slot.reshape(1, row_count), flat, *rows)
    return out.reshape(slots, parts, pair, LANES).transpose(0, 2, 1, 3).reshape(slots, pair, width)


def shift(values, distance):
    size = lax.axis_size("tensor")
    return lax.ppermute(values, "tensor", [(i, (i + distance) % size) for i in range(size)])


def gather_pieces(own):
    half = own.shape[0] // 2
    left = shift(own, 1)
    right = shift(own, -1)
    return own, left, right, shift(left[:half], 1), shift(right[half:], -1)


def rotary_tables(segment_ids):
    row_count = segment_ids.shape[0]
    row_ids = jnp.arange(row_count, dtype=i32)
    earlier = (segment_ids[:, None] == segment_ids[None, :]) & (row_ids[None, :] < row_ids[:, None])
    position = jnp.sum(earlier.astype(i32), axis=1)
    lane = jnp.arange(LANES, dtype=i32)
    exponent = (lane // 2).astype(f32) * (2.0 / ROT)
    inverse_freq = 1.0 / rotary_base**exponent
    angles = position.astype(f32)[:, None] * inverse_freq[None, :]
    turned = (lane < ROT)[None, :]
    sign = jnp.where(lane % 2 == 0, -1.0, 1.0)[None, :]
    return jnp.where(turned, jnp.cos(angles), 1.0), jnp.where(turned, jnp.sin(angles) * sign, 0.0)


def shards(
    stream,
    target_row,
    segment_ids,
    cache_slot,
    norm_gain,
    norm_bias,
    projection,
    output_weight,
    cache_pool,
):
    peers = lax.axis_size("req")
    groups = lax.axis_size("tensor")
    me = lax.axis_index("tensor")
    row_count, width = stream.shape
    depth = projection.shape[0]

    packed = pack(target_row, stream, peers)
    packed, projection, output_weight, segment_ids, cache_slot = lax.optimization_barrier(
        (packed, projection, output_weight, segment_ids, cache_slot)
    )
    got = lax.all_to_all(packed, "req", split_axis=0, concat_axis=0, tiled=True)

    weights = [projection[:, which, :] for which in range(3)]
    cosine, sine = rotary_tables(segment_ids)
    segment_row = segment_ids.reshape(1, row_count)
    segment_col = segment_ids.reshape(row_count, 1)
    live_slot = jnp.where(segment_ids >= 0, cache_slot, -1)
    gain = norm_gain.reshape(1, depth)
    bias = norm_bias.reshape(1, depth)
    out_weights = []
    for offset in range(groups):
        target = lax.rem(me + offset, groups)
        block = lax.dynamic_slice_in_dim(output_weight, target * width, width, axis=1)
        out_weights.append(block if offset == 0 else shift(block, offset))
    group = me.astype(i32).reshape(1)
    got, weights, cosine, sine, segment_col, out_weights = lax.optimization_barrier(
        (got, weights, cosine, sine, segment_col, out_weights)
    )

    placed = unpack(got, row_count, width)
    gathered = []
    for chunk in placed:
        if gathered:
            chunk, _ = lax.optimization_barrier((chunk, gathered[-1][1:3]))
        gathered.append(gather_pieces(chunk))
    keys, values, contexts = [], [], []
    for number in range(CHUNKS):
        context, key, value = layer(
            number, group, gathered[number], weights, gain, bias, cosine, sine, segment_row, segment_col, keys, values
        )
        keys.append(key)
        values.append(value)
        contexts.append(gather_pieces(context))
    mixed = None
    for number in range(CHUNKS):
        mixed = finish(number, contexts[number], out_weights, placed[number], segment_col, mixed)
    return (mixed, write_pool(live_slot, cache_pool, keys, values))


def solution(mesh):
    in_specs = (
        P("req", "tensor"),
        P("req"),
        P("req"),
        P("req"),
        P(),
        P(),
        P(None, None, "tensor"),
        P("tensor", None),
        P("req", None, "tensor"),
    )
    out_specs = (P("req", "tensor"), P("req", None, "tensor"))
    return jax.shard_map(shards, mesh=mesh, in_specs=in_specs, out_specs=out_specs, check_vma=False)
```

```python
import functools
import math

import jax
import jax.numpy as jnp
from jax import lax
from jax.experimental import pallas as pl
from jax.experimental.pallas import tpu as pltpu
from jax.sharding import PartitionSpec as P

HDIM = 256
ROT = 64
LANES = 128
CHUNKS = 2

norm_epsilon = 1e-05
masked_score = -1e30
rotary_base = 10000.0

bf16 = jnp.bfloat16
f32 = jnp.float32
i32 = jnp.int32


def iota(shape, dim):
    return lax.broadcasted_iota(i32, shape, dim)


def hot(condition):
    return jnp.where(condition, 1.0, 0.0).astype(bf16)


def dot(a, b):
    return jnp.dot(a, b, preferred_element_type=f32)


def dot_nt(a, b):
    return lax.dot_general(a, b, (((1,), (1,)), ((), ())), preferred_element_type=f32)


def whole(shape):
    zeros = (0,) * len(shape)
    return pl.BlockSpec(shape, lambda *_: zeros)


def pack_kernel(target_ref, stream_ref, packed_ref, *, peers):
    row_count = target_ref.shape[1]
    cap = row_count // peers
    width = stream_ref.shape[1]
    parts = width // LANES
    target = target_ref[...]
    sends = target >= 0
    receiver = jnp.where(sends, target // row_count, peers)
    local = jnp.where(sends, target - receiver * row_count + 1, 0)
    onehot = jnp.where(iota((peers, row_count), 0) == receiver, 1.0, 0.0)
    upper = hot(iota((LANES, LANES), 0) < iota((LANES, LANES), 1))
    carry = jnp.zeros((peers, 1), f32)
    ranks = []
    for start in range(0, row_count, LANES):
        block = onehot[:, start : start + LANES]
        before = dot(block.astype(bf16), upper) + carry
        ranks.append(jnp.sum(block * before, axis=0, keepdims=True))
        carry = carry + jnp.sum(block, axis=1, keepdims=True)
    rank = jnp.concatenate(ranks, axis=1).astype(i32)
    slot = jnp.where(sends, receiver * cap + rank, -1)
    high = local // 32
    low = local - high * 32
    lane = iota((LANES, row_count), 0)
    table = dot_nt((onehot * high.astype(f32)).astype(bf16), hot(lane == rank)) + dot_nt(
        (onehot * low.astype(f32)).astype(bf16), hot(lane == rank + cap)
    )
    repeat = hot(iota((peers * 8, peers), 0) // 8 == iota((peers * 8, peers), 1))
    packed_ref[:, cap * parts :, :] = (
        dot(repeat, table.astype(bf16)).reshape(peers, 8, LANES).astype(bf16)
    )
    step = 256
    for start in range(0, row_count, step):
        chosen = hot(iota((step, row_count), 0) + start == slot)
        rows = dot(chosen, stream_ref[...])
        first = start // cap
        for part in range(parts):
            packed_ref[first : first + step // cap, part * cap : (part + 1) * cap, :] = (
                rows[:, part * LANES : (part + 1) * LANES].reshape(step // cap, cap, LANES).astype(bf16)
            )


def pack(target, stream, peers):
    row_count, width = stream.shape
    cap = row_count // peers
    return pl.pallas_call(
        functools.partial(pack_kernel, peers=peers),
        out_shape=jax.ShapeDtypeStruct((peers, cap * (width // LANES) + 8, LANES), bf16),
        name="pack",
    )(target.reshape(1, row_count), stream)


def unpack_kernel(got_ref, *placed_refs):
    peers = got_ref.shape[0]
    chunk, width = placed_refs[0].shape
    row_count = chunk * len(placed_refs)
    cap = row_count // peers
    parts = width // LANES
    tables = got_ref[:, cap * parts :, :].astype(f32).reshape(peers * 8, LANES).astype(bf16)
    table = dot(hot(iota((peers, peers * 8), 1) == 8 * iota((peers, peers * 8), 0)), tables)
    table = table.astype(bf16)
    lane = iota((LANES, row_count), 0)
    rank = iota((LANES, row_count), 1) % cap
    value = 32.0 * dot(table, hot(lane == rank)) + dot(table, hot(lane == rank + cap))
    owner = iota((peers, row_count), 1) // cap == iota((peers, row_count), 0)
    arrived = jnp.sum(jnp.where(owner, value, 0.0), axis=0, keepdims=True).astype(i32) - 1
    for number, placed_ref in enumerate(placed_refs):
        chosen = hot(iota((chunk, row_count), 0) + number * chunk == arrived)
        for part in range(parts):
            rows = got_ref[:, part * cap : (part + 1) * cap, :].reshape(row_count, LANES)
            placed_ref[:, part * LANES : (part + 1) * LANES] = dot(chosen, rows).astype(bf16)


def unpack(got, row_count, width):
    chunk = row_count // CHUNKS
    return pl.pallas_call(
        unpack_kernel,
        out_shape=[jax.ShapeDtypeStruct((chunk, width), bf16)] * CHUNKS,
        name="unpack",
    )(got)


def layer_kernel(number, group_ref, *refs):
    own, left, right, far_top, far_bottom, *weights_from = refs[:8]
    cosine_from, sine_from, gain, bias, segment_row, segment_col = refs[8:14]
    past_keys = refs[14 : 14 + number]
    past_values = refs[14 + number : 14 + 2 * number]
    context, keys_out, values_out, pieces_ref, weights_ref, cosine, sine, done = refs[14 + 2 * number :]
    chunk, width = own.shape
    half = chunk // 2
    groups = gain.shape[1] // width
    me = group_ref[0]
    table_rows = pl.ds(number * chunk, chunk)
    moves = [
        (own, pieces_ref.at[0]),
        (left, pieces_ref.at[1]),
        (far_top, pieces_ref.at[2, pl.ds(0, half)]),
        (far_bottom, pieces_ref.at[2, pl.ds(half, half)]),
        (right, pieces_ref.at[3]),
        *[(source, weights_ref.at[which]) for which, source in enumerate(weights_from)],
        (cosine_from.at[table_rows], cosine),
        (sine_from.at[table_rows], sine),
    ]
    copies = [pltpu.make_async_copy(source, to, done.at[i]) for i, (source, to) in enumerate(moves)]
    for copy in copies:
        copy.start()
    for copy in copies[:5]:
        copy.wait()
    pieces = [pieces_ref[i].astype(f32) for i in range(4)]
    total = sum(jnp.sum(piece, axis=1, keepdims=True) for piece in pieces)
    mean = total * (1.0 / (width * groups))
    centred = [piece - mean for piece in pieces]
    spread = sum(jnp.sum(piece * piece, axis=1, keepdims=True) for piece in centred)
    scale = lax.rsqrt(spread * (1.0 / (width * groups)) + norm_epsilon)
    for copy in copies[5:]:
        copy.wait()
    projected = [0.0, 0.0, 0.0]
    for offset, piece in enumerate(centred):
        source = lax.rem(me + groups - offset, groups)
        place = pl.ds(pl.multiple_of(source * width, width), width)
        normed = (piece * scale * gain[:, place].astype(f32) + bias[:, place].astype(f32)).astype(bf16)
        projected = [total + dot(normed, weights_ref[i, place, :]) for i, total in enumerate(projected)]
    raw_queries, raw_keys, raw_values = [total.astype(bf16) for total in projected]
    cos_part = cosine[...]
    sin_part = sine[...]
    even = iota((chunk, LANES), 1) % 2 == 0

    def turn(head):
        lead = head[:, :LANES].astype(f32)
        swapped = jnp.where(even, pltpu.roll(lead, LANES - 1, 1), pltpu.roll(lead, 1, 1))
        turned = (lead * cos_part + swapped * sin_part).astype(bf16)
        return jnp.concatenate([turned, head[:, LANES:]], axis=1)

    segment = segment_col[...]
    allowed = []
    for block in range(number + 1):
        same = segment_row[:, block * chunk : (block + 1) * chunk] == segment
        if block == number:
            same = same & (iota((chunk, chunk), 1) <= iota((chunk, chunk), 0))
        allowed.append(same)
    score_scale = 1.0 / math.sqrt(HDIM)
    for head in range(width // HDIM):
        cols = slice(head * HDIM, (head + 1) * HDIM)
        query = turn(raw_queries[:, cols])
        key = turn(raw_keys[:, cols])
        value = raw_values[:, cols]
        keys_out[:, cols] = key
        values_out[:, cols] = value
        keys = [ref[:, cols] for ref in past_keys] + [key]
        values = [ref[:, cols] for ref in past_values] + [value]
        scores = [
            jnp.where(mask, dot_nt(query, block) * score_scale, masked_score)
            for mask, block in zip(allowed, keys)
        ]
        top = functools.reduce(jnp.maximum, [jnp.max(s, axis=1, keepdims=True) for s in scores])
        raised = [jnp.where(mask, jnp.exp(s - top), 0.0) for mask, s in zip(allowed, scores)]
        row_total = sum(jnp.sum(r, axis=1, keepdims=True) for r in raised)
        inverse = 1.0 / row_total
        mixed = sum(dot((r * inverse).astype(bf16), v) for r, v in zip(raised, values))
        context[:, cols] = mixed.astype(bf16)


def layer(number, group, pieces, weights, gain, bias, cosine, sine, segment_row, segment_col, keys, values):
    chunk, width = pieces[0].shape
    by_chunk = lambda columns: pl.BlockSpec((chunk, columns), lambda i, g: (number, 0))
    rows = jax.ShapeDtypeStruct((chunk, width), bf16)
    pieces, weights, cosine, sine = jax.tree.map(
        lambda array: pltpu.with_memory_space_constraint(array, pltpu.MemorySpace.HBM), (pieces, weights, cosine, sine)
    )
    return pl.pallas_call(
        functools.partial(layer_kernel, number),
        grid_spec=pltpu.PrefetchScalarGridSpec(
            num_scalar_prefetch=1,
            grid=(1,),
            in_specs=[pl.BlockSpec(memory_space=pltpu.MemorySpace.HBM)] * (len(pieces) + len(weights) + 2)
            + [whole(gain.shape), whole(bias.shape), whole(segment_row.shape), by_chunk(1)]
            + [whole(rows.shape)] * (2 * number),
            out_specs=[whole(rows.shape)] * 3,
            scratch_shapes=[
                pltpu.VMEM((4, chunk, width), bf16),
                pltpu.VMEM((len(weights), *weights[0].shape), bf16),
                pltpu.VMEM((chunk, LANES), f32),
                pltpu.VMEM((chunk, LANES), f32),
                pltpu.SemaphoreType.DMA((len(pieces) + len(weights) + 2,)),
            ],
        ),
        out_shape=[rows] * 3,
        compiler_params=pltpu.CompilerParams(vmem_limit_bytes=40 << 20),
        name="layer",
    )(group, *pieces, *weights, cosine, sine, gain, bias, segment_row, segment_col, *keys, *values)


def finish_kernel(*refs):
    own, left, right, far_top, far_bottom, w_own, w_left, w_far, w_right, placed, segment_col = refs[:11]
    mixed = refs[-1]
    total = dot(own[...], w_own[...]) + dot(left[...], w_left[...]) + dot(right[...], w_right[...])
    total = total + dot(jnp.concatenate([far_top[...], far_bottom[...]], axis=0), w_far[...])
    mixed[...] = jnp.where(segment_col[...] >= 0, placed[...].astype(f32) + total, 0.0).astype(bf16)


def finish(number, pieces, weights, placed, segment_col, buffer):
    chunk, width = placed.shape
    row_count = segment_col.shape[0]
    given = [*pieces, *weights, placed]
    specs = [whole(array.shape) for array in given] + [pl.BlockSpec((chunk, 1), lambda i: (number, 0))]
    given.append(segment_col)
    aliases = {}
    if buffer is not None:
        aliases = {len(given): 0}
        given.append(buffer)
        specs.append(pl.BlockSpec(memory_space=pl.ANY))
    return pl.pallas_call(
        finish_kernel,
        grid=(1,),
        in_specs=specs,
        out_specs=pl.BlockSpec((chunk, width), lambda i: (number, 0)),
        out_shape=jax.ShapeDtypeStruct((row_count, width), bf16),
        input_output_aliases=aliases,
        compiler_params=pltpu.CompilerParams(vmem_limit_bytes=16 << 20),
        name="finish",
    )(*given)


def pool_kernel(slot_ref, old_ref, *refs):
    *row_refs, out_ref, spread_ref = refs
    row_count = slot_ref.shape[1]
    half = len(row_refs) // 2
    width = row_refs[0].shape[1]
    parts = width // LANES
    chunk = row_refs[0].shape[0]
    per_slot = 2 * parts
    step = out_ref.shape[0] // per_slot
    chosen = hot(iota((step, row_count), 0) + pl.program_id(0) * step == slot_ref[...])
    found = jnp.sum(chosen.astype(f32), axis=1, keepdims=True)
    for which in range(2):
        rows = sum(
            dot(chosen[:, number * chunk : (number + 1) * chunk], ref[...])
            for number, ref in enumerate(row_refs[which * half : (which + 1) * half])
        )
        for part in range(parts):
            spread_ref[pl.ds(2 * part + which, step, stride=per_slot), :] = rows[
                :, part * LANES : (part + 1) * LANES
            ]
    repeat = hot(iota((step * per_slot, step), 0) // per_slot == iota((step * per_slot, step), 1))
    written = dot(repeat, jnp.broadcast_to(found, (step, LANES)).astype(bf16))
    out_ref[...] = jnp.where(written > 0.5, spread_ref[...].astype(bf16), old_ref[...])


def write_pool(live_slot, cache_pool, keys, values):
    slots, pair, width = cache_pool.shape
    parts = width // LANES
    per_slot = pair * parts
    step = 256
    row_count = live_slot.shape[0]
    flat = cache_pool.reshape(slots, pair, parts, LANES).transpose(0, 2, 1, 3).reshape(slots * per_slot, LANES)
    block = pl.BlockSpec((step * per_slot, LANES), lambda i: (i, 0))
    rows = [*keys, *values]
    out = pl.pallas_call(
        pool_kernel,
        grid=(slots // step,),
        in_specs=[whole((1, row_count)), block] + [whole(array.shape) for array in rows],
        out_specs=block,
        out_shape=jax.ShapeDtypeStruct(flat.shape, bf16),
        scratch_shapes=[pltpu.VMEM((step * per_slot, LANES), f32)],
        compiler_params=pltpu.CompilerParams(vmem_limit_bytes=32 << 20),
        name="pool",
    )(live_slot.reshape(1, row_count), flat, *rows)
    return out.reshape(slots, parts, pair, LANES).transpose(0, 2, 1, 3).reshape(slots, pair, width)


def shift(values, distance):
    size = lax.axis_size("tensor")
    return lax.ppermute(values, "tensor", [(i, (i + distance) % size) for i in range(size)])


def rotary_tables(segment_ids):
    row_count = segment_ids.shape[0]
    row_ids = jnp.arange(row_count, dtype=i32)
    earlier = (segment_ids[:, None] == segment_ids[None, :]) & (row_ids[None, :] < row_ids[:, None])
    position = jnp.sum(earlier.astype(i32), axis=1)
    lane = jnp.arange(LANES, dtype=i32)
    exponent = (lane // 2).astype(f32) * (2.0 / ROT)
    inverse_freq = 1.0 / rotary_base**exponent
    angles = position.astype(f32)[:, None] * inverse_freq[None, :]
    turned = (lane < ROT)[None, :]
    sign = jnp.where(lane % 2 == 0, -1.0, 1.0)[None, :]
    return jnp.where(turned, jnp.cos(angles), 1.0), jnp.where(turned, jnp.sin(angles) * sign, 0.0)


def shards(
    stream,
    target_row,
    segment_ids,
    cache_slot,
    norm_gain,
    norm_bias,
    projection,
    output_weight,
    cache_pool,
):
    peers = lax.axis_size("req")
    groups = lax.axis_size("tensor")
    me = lax.axis_index("tensor")
    row_count, width = stream.shape
    depth = projection.shape[0]

    packed = pack(target_row, stream, peers)
    packed, projection, output_weight, segment_ids, cache_slot = lax.optimization_barrier(
        (packed, projection, output_weight, segment_ids, cache_slot)
    )
    got = lax.all_to_all(packed, "req", split_axis=0, concat_axis=0, tiled=True)

    weights = [projection[:, which, :] for which in range(3)]
    cosine, sine = rotary_tables(segment_ids)
    segment_row = segment_ids.reshape(1, row_count)
    segment_col = segment_ids.reshape(row_count, 1)
    live_slot = jnp.where(segment_ids >= 0, cache_slot, -1)
    gain = norm_gain.reshape(1, depth)
    bias = norm_bias.reshape(1, depth)
    out_weights = []
    for offset in range(groups):
        target = lax.rem(me + offset, groups)
        block = lax.dynamic_slice_in_dim(output_weight, target * width, width, axis=1)
        out_weights.append(block if offset == 0 else shift(block, offset))
    group = me.astype(i32).reshape(1)
    got, weights, cosine, sine, segment_col, out_weights = lax.optimization_barrier(
        (got, weights, cosine, sine, segment_col, out_weights)
    )

    placed = unpack(got, row_count, width)
    own, later = placed
    half = own.shape[0] // 2
    layer_args = (weights, gain, bias, cosine, sine, segment_row, segment_col)

    def near(rows):
        return shift(rows, 1), shift(rows, -1)

    def far(left, right):
        return shift(left, 1), shift(right, -1)

    left0, right0 = near(own)
    left0_half, right0_half, later = lax.optimization_barrier((left0[:half], right0[half:], later))
    far0 = far(left0_half, right0_half)
    left1, right1 = near(later)
    context0, key0, value0 = layer(0, group, (own, left0, right0, *far0), *layer_args, [], [])
    far1 = far(left1[:half], right1[half:])
    *far1, context0 = lax.optimization_barrier((*far1, context0))
    context_left0, context_right0 = near(context0)
    context1, key1, value1 = layer(1, group, (later, left1, right1, *far1), *layer_args, [key0], [value0])
    context_left0, context_right0, context1 = lax.optimization_barrier((context_left0, context_right0, context1))
    context_far0 = far(context_left0[:half], context_right0[half:])
    context_left1, context_right1 = near(context1)
    new_pool = write_pool(live_slot, cache_pool, [key0, key1], [value0, value1])
    context_left1, context_right1, new_pool = lax.optimization_barrier((context_left1, context_right1, new_pool))
    context_far1 = far(context_left1[:half], context_right1[half:])
    mixed = finish(0, (context0, context_left0, context_right0, *context_far0), out_weights, own, segment_col, None)
    mixed = finish(1, (context1, context_left1, context_right1, *context_far1), out_weights, later, segment_col, mixed)
    return (mixed, new_pool)


def solution(mesh):
    in_specs = (
        P("req", "tensor"),
        P("req"),
        P("req"),
        P("req"),
        P(),
        P(),
        P(None, None, "tensor"),
        P("tensor", None),
        P("req", None, "tensor"),
    )
    out_specs = (P("req", "tensor"), P("req", None, "tensor"))
    return jax.shard_map(shards, mesh=mesh, in_specs=in_specs, out_specs=out_specs, check_vma=False)
```

```python
import functools
import math

import jax
import jax.numpy as jnp
from jax import lax
from jax.experimental import pallas as pl
from jax.experimental.pallas import tpu as pltpu
from jax.sharding import PartitionSpec as P

HDIM = 256
ROT = 64
LANES = 128
CHUNKS = 2

norm_epsilon = 1e-05
masked_score = -1e30
rotary_base = 10000.0

bf16 = jnp.bfloat16
f32 = jnp.float32
i32 = jnp.int32


def iota(shape, dim):
    return lax.broadcasted_iota(i32, shape, dim)


def hot(condition):
    return jnp.where(condition, 1.0, 0.0).astype(bf16)


def dot(a, b):
    return jnp.dot(a, b, preferred_element_type=f32)


def dot_nt(a, b):
    return lax.dot_general(a, b, (((1,), (1,)), ((), ())), preferred_element_type=f32)


def whole(shape):
    zeros = (0,) * len(shape)
    return pl.BlockSpec(shape, lambda *_: zeros)


def pack_kernel(target_ref, stream_ref, packed_ref, *, peers):
    row_count = target_ref.shape[1]
    cap = row_count // peers
    width = stream_ref.shape[1]
    parts = width // LANES
    target = target_ref[...]
    sends = target >= 0
    receiver = jnp.where(sends, target // row_count, peers)
    local = jnp.where(sends, target - receiver * row_count + 1, 0)
    onehot = jnp.where(iota((peers, row_count), 0) == receiver, 1.0, 0.0)
    upper = hot(iota((LANES, LANES), 0) < iota((LANES, LANES), 1))
    carry = jnp.zeros((peers, 1), f32)
    ranks = []
    for start in range(0, row_count, LANES):
        block = onehot[:, start : start + LANES]
        before = dot(block.astype(bf16), upper) + carry
        ranks.append(jnp.sum(block * before, axis=0, keepdims=True))
        carry = carry + jnp.sum(block, axis=1, keepdims=True)
    rank = jnp.concatenate(ranks, axis=1).astype(i32)
    slot = jnp.where(sends, receiver * cap + rank, -1)
    high = local // 32
    low = local - high * 32
    lane = iota((LANES, row_count), 0)
    table = dot_nt((onehot * high.astype(f32)).astype(bf16), hot(lane == rank)) + dot_nt(
        (onehot * low.astype(f32)).astype(bf16), hot(lane == rank + cap)
    )
    repeat = hot(iota((peers * 8, peers), 0) // 8 == iota((peers * 8, peers), 1))
    packed_ref[:, cap * parts :, :] = (
        dot(repeat, table.astype(bf16)).reshape(peers, 8, LANES).astype(bf16)
    )
    step = 256
    for start in range(0, row_count, step):
        chosen = hot(iota((step, row_count), 0) + start == slot)
        rows = dot(chosen, stream_ref[...])
        first = start // cap
        for part in range(parts):
            packed_ref[first : first + step // cap, part * cap : (part + 1) * cap, :] = (
                rows[:, part * LANES : (part + 1) * LANES].reshape(step // cap, cap, LANES).astype(bf16)
            )


def pack(target, stream, peers):
    row_count, width = stream.shape
    cap = row_count // peers
    return pl.pallas_call(
        functools.partial(pack_kernel, peers=peers),
        out_shape=jax.ShapeDtypeStruct((peers, cap * (width // LANES) + 8, LANES), bf16),
        name="pack",
    )(target.reshape(1, row_count), stream)


def unpack_kernel(got_ref, *placed_refs):
    peers = got_ref.shape[0]
    chunk, width = placed_refs[0].shape
    row_count = chunk * len(placed_refs)
    cap = row_count // peers
    parts = width // LANES
    tables = got_ref[:, cap * parts :, :].astype(f32).reshape(peers * 8, LANES).astype(bf16)
    table = dot(hot(iota((peers, peers * 8), 1) == 8 * iota((peers, peers * 8), 0)), tables)
    table = table.astype(bf16)
    lane = iota((LANES, row_count), 0)
    rank = iota((LANES, row_count), 1) % cap
    value = 32.0 * dot(table, hot(lane == rank)) + dot(table, hot(lane == rank + cap))
    owner = iota((peers, row_count), 1) // cap == iota((peers, row_count), 0)
    arrived = jnp.sum(jnp.where(owner, value, 0.0), axis=0, keepdims=True).astype(i32) - 1
    for number, placed_ref in enumerate(placed_refs):
        chosen = hot(iota((chunk, row_count), 0) + number * chunk == arrived)
        for part in range(parts):
            rows = got_ref[:, part * cap : (part + 1) * cap, :].reshape(row_count, LANES)
            placed_ref[:, part * LANES : (part + 1) * LANES] = dot(chosen, rows).astype(bf16)


def unpack(got, row_count, width):
    chunk = row_count // CHUNKS
    return pl.pallas_call(
        unpack_kernel,
        out_shape=[jax.ShapeDtypeStruct((chunk, width), bf16)] * CHUNKS,
        name="unpack",
    )(got)


def layer_kernel(number, group_ref, *refs):
    own, left, right, far_top, far_bottom, *weights_from = refs[:8]
    cosine_from, sine_from, gain, bias, segment_row, segment_col = refs[8:14]
    past_keys = refs[14 : 14 + number]
    past_values = refs[14 + number : 14 + 2 * number]
    context, keys_out, values_out, pieces_ref, weights_ref, cosine, sine, done = refs[14 + 2 * number :]
    chunk, width = own.shape
    half = chunk // 2
    groups = gain.shape[1] // width
    me = group_ref[0]
    table_rows = pl.ds(number * chunk, chunk)
    moves = [
        (own, pieces_ref.at[0]),
        (left, pieces_ref.at[1]),
        (far_top, pieces_ref.at[2, pl.ds(0, half)]),
        (far_bottom, pieces_ref.at[2, pl.ds(half, half)]),
        (right, pieces_ref.at[3]),
        *[(source, weights_ref.at[which]) for which, source in enumerate(weights_from)],
        (cosine_from.at[table_rows], cosine),
        (sine_from.at[table_rows], sine),
    ]
    copies = [pltpu.make_async_copy(source, to, done.at[i]) for i, (source, to) in enumerate(moves)]
    for copy in copies:
        copy.start()
    for copy in copies[:5]:
        copy.wait()
    pieces = [pieces_ref[i].astype(f32) for i in range(4)]
    total = sum(jnp.sum(piece, axis=1, keepdims=True) for piece in pieces)
    mean = total * (1.0 / (width * groups))
    centred = [piece - mean for piece in pieces]
    spread = sum(jnp.sum(piece * piece, axis=1, keepdims=True) for piece in centred)
    scale = lax.rsqrt(spread * (1.0 / (width * groups)) + norm_epsilon)
    for copy in copies[5:]:
        copy.wait()
    projected = [0.0, 0.0, 0.0]
    for offset, piece in enumerate(centred):
        source = lax.rem(me + groups - offset, groups)
        place = pl.ds(pl.multiple_of(source * width, width), width)
        normed = (piece * scale * gain[:, place].astype(f32) + bias[:, place].astype(f32)).astype(bf16)
        projected = [total + dot(normed, weights_ref[i, place, :]) for i, total in enumerate(projected)]
    raw_queries, raw_keys, raw_values = [total.astype(bf16) for total in projected]
    cos_part = cosine[...]
    sin_part = sine[...]
    even = iota((chunk, LANES), 1) % 2 == 0

    def turn(head):
        lead = head[:, :LANES].astype(f32)
        swapped = jnp.where(even, pltpu.roll(lead, LANES - 1, 1), pltpu.roll(lead, 1, 1))
        turned = (lead * cos_part + swapped * sin_part).astype(bf16)
        return jnp.concatenate([turned, head[:, LANES:]], axis=1)

    segment = segment_col[...]
    allowed = []
    for block in range(number + 1):
        same = segment_row[:, block * chunk : (block + 1) * chunk] == segment
        if block == number:
            same = same & (iota((chunk, chunk), 1) <= iota((chunk, chunk), 0))
        allowed.append(same)
    score_scale = 1.0 / math.sqrt(HDIM)
    for head in range(width // HDIM):
        cols = slice(head * HDIM, (head + 1) * HDIM)
        query = turn(raw_queries[:, cols])
        key = turn(raw_keys[:, cols])
        value = raw_values[:, cols]
        keys_out[:, cols] = key
        values_out[:, cols] = value
        keys = [ref[:, cols] for ref in past_keys] + [key]
        values = [ref[:, cols] for ref in past_values] + [value]
        scores = [
            jnp.where(mask, dot_nt(query, block) * score_scale, masked_score)
            for mask, block in zip(allowed, keys)
        ]
        top = functools.reduce(jnp.maximum, [jnp.max(s, axis=1, keepdims=True) for s in scores])
        raised = [jnp.where(mask, jnp.exp(s - top), 0.0) for mask, s in zip(allowed, scores)]
        row_total = sum(jnp.sum(r, axis=1, keepdims=True) for r in raised)
        inverse = 1.0 / row_total
        mixed = sum(dot((r * inverse).astype(bf16), v) for r, v in zip(raised, values))
        context[:, cols] = mixed.astype(bf16)


def layer(number, group, pieces, weights, gain, bias, cosine, sine, segment_row, segment_col, keys, values):
    chunk, width = pieces[0].shape
    by_chunk = lambda columns: pl.BlockSpec((chunk, columns), lambda i, g: (number, 0))
    rows = jax.ShapeDtypeStruct((chunk, width), bf16)
    pieces, weights, cosine, sine = jax.tree.map(
        lambda array: pltpu.with_memory_space_constraint(array, pltpu.MemorySpace.HBM), (pieces, weights, cosine, sine)
    )
    return pl.pallas_call(
        functools.partial(layer_kernel, number),
        grid_spec=pltpu.PrefetchScalarGridSpec(
            num_scalar_prefetch=1,
            grid=(1,),
            in_specs=[pl.BlockSpec(memory_space=pltpu.MemorySpace.HBM)] * (len(pieces) + len(weights) + 2)
            + [whole(gain.shape), whole(bias.shape), whole(segment_row.shape), by_chunk(1)]
            + [whole(rows.shape)] * (2 * number),
            out_specs=[whole(rows.shape)] * 3,
            scratch_shapes=[
                pltpu.VMEM((4, chunk, width), bf16),
                pltpu.VMEM((len(weights), *weights[0].shape), bf16),
                pltpu.VMEM((chunk, LANES), f32),
                pltpu.VMEM((chunk, LANES), f32),
                pltpu.SemaphoreType.DMA((len(pieces) + len(weights) + 2,)),
            ],
        ),
        out_shape=[rows] * 3,
        compiler_params=pltpu.CompilerParams(vmem_limit_bytes=40 << 20),
        name="layer",
    )(group, *pieces, *weights, cosine, sine, gain, bias, segment_row, segment_col, *keys, *values)


def finish_kernel(*refs):
    own, left, right, far_top, far_bottom, w_own, w_left, w_far, w_right, placed, segment_col = refs[:11]
    mixed = refs[-1]
    total = dot(own[...], w_own[...]) + dot(left[...], w_left[...]) + dot(right[...], w_right[...])
    total = total + dot(jnp.concatenate([far_top[...], far_bottom[...]], axis=0), w_far[...])
    mixed[...] = jnp.where(segment_col[...] >= 0, placed[...].astype(f32) + total, 0.0).astype(bf16)


def finish(number, pieces, weights, placed, segment_col, buffer):
    chunk, width = placed.shape
    row_count = segment_col.shape[0]
    given = [*pieces, *weights, placed]
    specs = [whole(array.shape) for array in given] + [pl.BlockSpec((chunk, 1), lambda i: (number, 0))]
    given.append(segment_col)
    aliases = {}
    if buffer is not None:
        aliases = {len(given): 0}
        given.append(buffer)
        specs.append(pl.BlockSpec(memory_space=pl.ANY))
    return pl.pallas_call(
        finish_kernel,
        grid=(1,),
        in_specs=specs,
        out_specs=pl.BlockSpec((chunk, width), lambda i: (number, 0)),
        out_shape=jax.ShapeDtypeStruct((row_count, width), bf16),
        input_output_aliases=aliases,
        compiler_params=pltpu.CompilerParams(vmem_limit_bytes=16 << 20),
        name="finish",
    )(*given)


def pool_kernel(slot_ref, old_ref, *refs):
    *row_refs, out_ref, spread_ref = refs
    row_count = slot_ref.shape[1]
    half = len(row_refs) // 2
    width = row_refs[0].shape[1]
    parts = width // LANES
    chunk = row_refs[0].shape[0]
    per_slot = 2 * parts
    step = out_ref.shape[0] // per_slot
    chosen = hot(iota((step, row_count), 0) + pl.program_id(0) * step == slot_ref[...])
    found = jnp.sum(chosen.astype(f32), axis=1, keepdims=True)
    for which in range(2):
        rows = sum(
            dot(chosen[:, number * chunk : (number + 1) * chunk], ref[...])
            for number, ref in enumerate(row_refs[which * half : (which + 1) * half])
        )
        for part in range(parts):
            spread_ref[pl.ds(2 * part + which, step, stride=per_slot), :] = rows[
                :, part * LANES : (part + 1) * LANES
            ]
    repeat = hot(iota((step * per_slot, step), 0) // per_slot == iota((step * per_slot, step), 1))
    written = dot(repeat, jnp.broadcast_to(found, (step, LANES)).astype(bf16))
    out_ref[...] = jnp.where(written > 0.5, spread_ref[...].astype(bf16), old_ref[...])


def write_pool(live_slot, cache_pool, keys, values):
    slots, pair, width = cache_pool.shape
    parts = width // LANES
    per_slot = pair * parts
    step = 256
    row_count = live_slot.shape[0]
    flat = cache_pool.reshape(slots, pair, parts, LANES).transpose(0, 2, 1, 3).reshape(slots * per_slot, LANES)
    block = pl.BlockSpec((step * per_slot, LANES), lambda i: (i, 0))
    rows = [*keys, *values]
    out = pl.pallas_call(
        pool_kernel,
        grid=(slots // step,),
        in_specs=[whole((1, row_count)), block] + [whole(array.shape) for array in rows],
        out_specs=block,
        out_shape=jax.ShapeDtypeStruct(flat.shape, bf16),
        scratch_shapes=[pltpu.VMEM((step * per_slot, LANES), f32)],
        compiler_params=pltpu.CompilerParams(vmem_limit_bytes=32 << 20),
        name="pool",
    )(live_slot.reshape(1, row_count), flat, *rows)
    return out.reshape(slots, parts, pair, LANES).transpose(0, 2, 1, 3).reshape(slots, pair, width)


def shift(values, distance):
    size = lax.axis_size("tensor")
    return lax.ppermute(values, "tensor", [(i, (i + distance) % size) for i in range(size)])


def rotary_tables(segment_ids):
    row_count = segment_ids.shape[0]
    row_ids = jnp.arange(row_count, dtype=i32)
    earlier = (segment_ids[:, None] == segment_ids[None, :]) & (row_ids[None, :] < row_ids[:, None])
    position = jnp.sum(earlier.astype(i32), axis=1)
    lane = jnp.arange(LANES, dtype=i32)
    exponent = (lane // 2).astype(f32) * (2.0 / ROT)
    inverse_freq = 1.0 / rotary_base**exponent
    angles = position.astype(f32)[:, None] * inverse_freq[None, :]
    turned = (lane < ROT)[None, :]
    sign = jnp.where(lane % 2 == 0, -1.0, 1.0)[None, :]
    return jnp.where(turned, jnp.cos(angles), 1.0), jnp.where(turned, jnp.sin(angles) * sign, 0.0)


def shards(
    stream,
    target_row,
    segment_ids,
    cache_slot,
    norm_gain,
    norm_bias,
    projection,
    output_weight,
    cache_pool,
):
    peers = lax.axis_size("req")
    groups = lax.axis_size("tensor")
    me = lax.axis_index("tensor")
    row_count, width = stream.shape
    depth = projection.shape[0]

    packed = pack(target_row, stream, peers)
    packed, projection, output_weight, segment_ids, cache_slot = lax.optimization_barrier(
        (packed, projection, output_weight, segment_ids, cache_slot)
    )
    got = lax.all_to_all(packed, "req", split_axis=0, concat_axis=0, tiled=True)

    weights = [projection[:, which, :] for which in range(3)]
    cosine, sine = rotary_tables(segment_ids)
    segment_row = segment_ids.reshape(1, row_count)
    segment_col = segment_ids.reshape(row_count, 1)
    live_slot = jnp.where(segment_ids >= 0, cache_slot, -1)
    gain = norm_gain.reshape(1, depth)
    bias = norm_bias.reshape(1, depth)
    out_weights = []
    for offset in range(groups):
        target = lax.rem(me + offset, groups)
        block = lax.dynamic_slice_in_dim(output_weight, target * width, width, axis=1)
        out_weights.append(block if offset == 0 else shift(block, offset))
    group = me.astype(i32).reshape(1)
    got, weights, cosine, sine, segment_col, out_weights = lax.optimization_barrier(
        (got, weights, cosine, sine, segment_col, out_weights)
    )

    placed = unpack(got, row_count, width)
    own, later = placed
    half = own.shape[0] // 2
    layer_args = (weights, gain, bias, cosine, sine, segment_row, segment_col)

    def near(rows):
        return shift(rows, 1), shift(rows, -1)

    def far(left, right):
        return shift(left, 1), shift(right, -1)

    left0, right0 = near(own)
    left0_half, right0_half, later = lax.optimization_barrier((left0[:half], right0[half:], later))
    far0 = far(left0_half, right0_half)
    left1, right1 = near(later)
    context0, key0, value0 = layer(0, group, (own, left0, right0, *far0), *layer_args, [], [])
    far1 = far(left1[:half], right1[half:])
    *far1, context0 = lax.optimization_barrier((*far1, context0))
    context_left0, context_right0 = near(context0)
    context1, key1, value1 = layer(1, group, (later, left1, right1, *far1), *layer_args, [key0], [value0])
    context_left0, context_right0, context1 = lax.optimization_barrier((context_left0, context_right0, context1))
    context_left0_half, context_right0_half, value1 = lax.optimization_barrier(
        (context_left0[:half], context_right0[half:], value1)
    )
    context_far0 = far(context_left0_half, context_right0_half)
    context_left1, context_right1 = near(context1)
    new_pool = write_pool(live_slot, cache_pool, [key0, key1], [value0, value1])
    context_left1, context_right1, new_pool = lax.optimization_barrier((context_left1, context_right1, new_pool))
    context_far1 = far(context_left1[:half], context_right1[half:])
    mixed = finish(0, (context0, context_left0, context_right0, *context_far0), out_weights, own, segment_col, None)
    mixed = finish(1, (context1, context_left1, context_right1, *context_far1), out_weights, later, segment_col, mixed)
    return (mixed, new_pool)


def solution(mesh):
    in_specs = (
        P("req", "tensor"),
        P("req"),
        P("req"),
        P("req"),
        P(),
        P(),
        P(None, None, "tensor"),
        P("tensor", None),
        P("req", None, "tensor"),
    )
    out_specs = (P("req", "tensor"), P("req", None, "tensor"))
    return jax.shard_map(shards, mesh=mesh, in_specs=in_specs, out_specs=out_specs, check_vma=False)
```
